256 devices in a mesh: layer: 16 (over y, x_hi, core), feat: 16 (over x_lo, z).
Axes of the slice: x: 4 (x_hi: 2, x_lo: 2; x = x_hi * 2 + x_lo), y: 4, z: 8, core: 2. Of those that a mesh axis runs over, the one named last changes fastest.
Arguments:
- pre_acts: bfloat16 [16, 512, 2048], P('layer', None, 'feat'), may hold values from -6 to 6
- decoder: bfloat16 [16, 16, 2048, 2048], P('layer', None, 'feat'), may hold values from -0.046875 to 0.046875
- dec_bias: bfloat16 [16, 2048], P('layer', 'feat'), may hold values from -3 to 3
- target: bfloat16 [16, 512, 2048], P('layer', None, 'feat'), may hold values from -6 to 6
Outputs:
- recon_error: float32 [16, 512, 2048], P('layer', None, 'feat')
- pre_grad: float32 [16, 512, 2048], P('layer', None, 'feat')
The draws below stay inside these ranges and needn't reach their ends.
All inputs are finite; a program needn't handle non-finite values.
Results may differ from the reference program's by a relative error of at most 0.015.
Values may be sent and summed in bfloat16 or wider, within the bound.
No kernel may reach another device: no remote copies, remote signals or barrier semaphores. Data moves between devices by JAX's collectives and lax.ppermute only.
A program may use at most 64 MiB of HBM per device.

```python
import jax
import jax.numpy as jnp
from jax import lax

D = 2048
FEAT_DEV = 128
TOKENS = 512
LAYERS = 16
FEATURES = 2048
N_FEAT = 16


def shard_levels(rng, dims, split, smallest, high):
    loudness, own = 1.0, jax.random.fold_in(rng, 6)
    for dim, parts in split:
        heights = jnp.exp(jax.random.uniform(jax.random.fold_in(own, dim), (parts,), jnp.float32, smallest / len(split), high / len(split)))
        loudness = loudness * jnp.repeat(heights, dims[dim] // parts).reshape([-1 if axis == dim else 1 for axis in range(len(dims))])
    return loudness


def noise(key, shape, scale, limit, split=(), kind=jnp.bfloat16):
    entries = jax.random.normal(key, shape, jnp.float32) * scale
    if len(split) > 0:
        entries = shard_levels(key, shape, split, -0.22, 0.18) * entries
    return jnp.clip(entries, min=-limit, max=limit).astype(kind)


def setup_inputs(seed: int = 0) -> dict:
    seeds = jax.random.split(jax.random.key(seed), 5)
    pre_acts = noise(seeds[0], (LAYERS, TOKENS, FEATURES), 1.0, 6.0, ((0, 16), (2, 16)))
    decoder = noise(seeds[1], (LAYERS, LAYERS, FEATURES, D), (FEATURES * LAYERS // 2) ** -0.5, 0.046875, ((0, 16), (2, 16)))
    dec_bias = noise(seeds[2], (LAYERS, D), 0.5, 3.0, ((0, 16), (1, 16)))
    target = noise(seeds[3], (LAYERS, TOKENS, D), 1.0, 6.0, ((0, 16), (2, 16)))
    return {"pre_acts": pre_acts, "decoder": decoder, "dec_bias": dec_bias, "target": target}


def rounded(value):
    return lax.optimization_barrier(value.astype(jnp.bfloat16)).astype(jnp.float32)


def reference(pre_acts, decoder, dec_bias, target):
    token_count = pre_acts.shape[1]
    activations = jnp.maximum(pre_acts, jnp.zeros((), pre_acts.dtype)).astype(jnp.float32)
    blocked = activations.reshape(LAYERS, token_count, N_FEAT, FEAT_DEV)
    errors = []
    for target_layer in range(LAYERS):
        partial_value = jnp.zeros((N_FEAT, token_count, D), jnp.float32)
        for source_layer in range(target_layer + 1):
            weights = decoder[target_layer, source_layer].astype(jnp.float32).reshape(N_FEAT, FEAT_DEV, D)
            partial_value = partial_value + jnp.einsum("nbf,bfd->bnd", blocked[source_layer], weights)
        summed = jnp.sum(rounded(partial_value), axis=0)
        errors.append(summed + dec_bias[target_layer].astype(jnp.float32)[None, :] - target[target_layer].astype(jnp.float32))
    recon_error = jnp.stack(errors)
    error_rounded = rounded(recon_error)
    grads = []
    for source_layer in range(LAYERS):
        running = jnp.zeros((token_count, FEATURES), jnp.float32)
        for target_layer in range(source_layer, LAYERS):
            weights = decoder[target_layer, source_layer].astype(jnp.float32)
            product = jnp.einsum("nd,fd->nf", error_rounded[target_layer], weights)
            running = running + rounded(product)
        grads.append(running * (pre_acts[source_layer] > 0).astype(jnp.float32))
    return recon_error, jnp.stack(grads)
```

```python
import jax
import jax.numpy as jnp
from jax import lax
from jax.experimental import pallas as pl
from jax.experimental.pallas import tpu as pltpu
from jax.sharding import Mesh
from jax.sharding import PartitionSpec as P


LAYER = ("y", "xh", "c")
FEAT = ("xl", "z")
NZ = 8
NS = 16
BLK = 128
ORDER = (
    (1, -3), (1, 3), (1, 4), (0, 4),
    (1, 2), (1, -2), (0, -3), (0, 3),
    (1, 1), (0, -2), (0, 2), (1, -1),
    (0, -1), (0, 1), (1, 0), (0, 0),
)


def place():
    layer = (lax.axis_index("y") * 2 + lax.axis_index("xh")) * 2 + lax.axis_index("c")
    return layer, lax.axis_index("c"), lax.axis_index("xl"), lax.axis_index("z")


def block_of(xl, z, flip, shift):
    return lax.rem(xl + flip, 2) * NZ + lax.rem(z + shift + NZ, NZ)


def columns(block):
    return pl.ds(pl.multiple_of(block * BLK, BLK), BLK)


def forward_kernel(same_ref, other_ref, w_ref, *rest):
    outs = rest[:NS]
    x_ref, w_vmem, sems = rest[NS:]
    layer, core, xl, z = place()

    def fetch(pair, half):
        flip, shift = ORDER[2 * pair + half]
        return pltpu.make_async_copy(
            w_ref.at[:, :, columns(block_of(xl, z, flip, shift))],
            w_vmem.at[pair, :, :, pl.ds(half * BLK, BLK)],
            sems.at[pair, half],
        )

    for pair in range(NS // 2):
        for half in range(2):
            fetch(pair, half).start()
    for j in range(NS // 2):
        for source, ref in ((2 * j + core, same_ref), (2 * j + 1 - core, other_ref)):
            rows = ref[j]
            x_ref[:, columns(source)] = jnp.where(source <= layer, rows, jnp.zeros_like(rows))
    for pair in range(NS // 2):
        fetch(pair, 0).wait()
        fetch(pair, 1).wait()
        w = w_vmem[pair].reshape(NS * BLK, 2 * BLK)
        value = jnp.dot(x_ref[...], w, preferred_element_type=jnp.float32).astype(jnp.bfloat16)
        outs[2 * pair][...] = value[:, :BLK]
        outs[2 * pair + 1][...] = value[:, BLK:]


def forward(same, other, w):
    tokens = same.shape[1]
    whole = pl.BlockSpec(memory_space=pltpu.VMEM)
    return pl.pallas_call(
        forward_kernel,
        out_shape=[jax.ShapeDtypeStruct((tokens, BLK), jnp.bfloat16)] * NS,
        in_specs=[whole, whole, pl.BlockSpec(memory_space=pl.ANY)],
        out_specs=[whole] * NS,
        scratch_shapes=[
            pltpu.VMEM((tokens, NS * BLK), jnp.bfloat16),
            pltpu.VMEM((NS // 2, NS, BLK, 2 * BLK), jnp.bfloat16),
            pltpu.SemaphoreType.DMA((NS // 2, 2)),
        ],
        cost_estimate=pl.CostEstimate(flops=2 * tokens * 2048 * 2048, bytes_accessed=12 << 20, transcendentals=0),
        name="forward",
    )(same, other, w)


def backward_kernel(*refs):
    blocks = refs[:NS]
    w_ref, send_ref, keep_ref, e_ref, w_vmem, sems = refs[NS:]
    layer, core, xl, z = place()

    def fetch(i):
        source = 2 * i + 1 - core if i < NS // 2 else 2 * (i - NS // 2) + core
        return pltpu.make_async_copy(w_ref.at[source], w_vmem.at[i], sems.at[i])

    for i in range(NS):
        fetch(i).start()
    for (flip, shift), ref in zip(ORDER, blocks):
        e_ref[:, columns(block_of(xl, z, flip, shift))] = ref[...]
    for pair in range(NS // 2):
        fetch(2 * pair).wait()
        fetch(2 * pair + 1).wait()
        w = w_vmem[pl.ds(2 * pair, 2)].reshape(2 * BLK, NS * BLK)
        value = lax.dot_general(
            e_ref[...], w, (((1,), (1,)), ((), ())), preferred_element_type=jnp.float32
        )
        for half in range(2):
            i = 2 * pair + half
            j = i % (NS // 2)
            source, ref = (2 * j + 1 - core, send_ref) if i < NS // 2 else (2 * j + core, keep_ref)
            term = value[:, half * BLK : (half + 1) * BLK]
            ref[j] = jnp.where(source <= layer, term, jnp.zeros_like(term)).astype(jnp.bfloat16)


def backward(blocks, w):
    tokens = blocks[0].shape[0]
    whole = pl.BlockSpec(memory_space=pltpu.VMEM)
    return pl.pallas_call(
        backward_kernel,
        out_shape=[jax.ShapeDtypeStruct((NS // 2, tokens, BLK), jnp.bfloat16)] * 2,
        in_specs=[whole] * NS + [pl.BlockSpec(memory_space=pl.ANY)],
        out_specs=[whole] * 2,
        scratch_shapes=[
            pltpu.VMEM((tokens, NS * BLK), jnp.bfloat16),
            pltpu.VMEM((NS, BLK, NS * BLK), jnp.bfloat16),
            pltpu.SemaphoreType.DMA((NS,)),
        ],
        cost_estimate=pl.CostEstimate(flops=2 * tokens * 2048 * 2048, bytes_accessed=12 << 20, transcendentals=0),
        name="backward",
    )(*blocks, w)


def to_feat(x, flip, shift):
    perm = [(a * NZ + z, (a + flip) % 2 * NZ + (z + shift) % NZ) for a in range(2) for z in range(NZ)]
    return lax.ppermute(x, FEAT, perm)


def swap_cores(x):
    return lax.ppermute(x, "c", [(0, 1), (1, 0)])


def add(*values):
    total = values[0].astype(jnp.float32)
    for value in values[1:]:
        total = total + value.astype(jnp.float32)
    return total


def narrow(x):
    return x.astype(jnp.bfloat16)


def reduce_over_feat(part):
    s, o = (lambda k: part[0, k]), (lambda k: part[1, k])
    a1 = to_feat(o(-3), 0, -1)
    a2 = to_feat(o(3), 0, 1)
    a3 = to_feat(o(4), 1, 0)
    b1 = to_feat(narrow(add(s(4), a3)), 0, -1)
    b2 = to_feat(narrow(add(o(2), a2)), 0, 1)
    b3 = to_feat(narrow(add(o(-2), a1)), 1, 0)
    c1 = to_feat(narrow(add(s(-3), b1)), 0, -1)
    c2 = to_feat(s(3), 0, 1)
    c3 = to_feat(narrow(add(o(1), b2)), 1, 0)
    d1 = to_feat(narrow(add(s(-2), b3, c1)), 0, -1)
    d2 = to_feat(narrow(add(s(2), c2)), 0, 1)
    d3 = to_feat(o(-1), 1, 0)
    e1 = to_feat(narrow(add(s(-1), d3, d1)), 0, -1)
    e2 = to_feat(narrow(add(s(1), c3, d2)), 0, 1)
    e3 = to_feat(o(0), 1, 0)
    return add(s(0), e1, e2, e3)


def gather_over_feat(x):
    g = {(0, 0): x}
    g[0, -1], g[0, 1], g[1, 0] = to_feat(x, 0, 1), to_feat(x, 0, -1), to_feat(x, 1, 0)
    g[0, -2], g[0, 2], g[1, -1] = to_feat(g[0, -1], 0, 1), to_feat(g[0, 1], 0, -1), to_feat(g[0, -1], 1, 0)
    g[0, -3], g[0, 3], g[1, 1] = to_feat(g[0, -2], 0, 1), to_feat(g[0, 2], 0, -1), to_feat(g[0, 1], 1, 0)
    g[0, 4], g[1, 2], g[1, -2] = to_feat(g[0, -3], 0, 1), to_feat(g[1, 1], 0, -1), to_feat(g[0, -2], 1, 0)
    g[1, -3], g[1, 3], g[1, 4] = to_feat(g[1, -2], 0, 1), to_feat(g[1, 2], 0, -1), to_feat(g[0, 4], 1, 0)
    return [g[key] for key in ORDER]


def on_device(pre_acts, decoder, dec_bias, target):
    w = decoder[0]
    pre = pre_acts[0]
    activations = jnp.maximum(pre, jnp.zeros((), pre.dtype))
    copies = jnp.broadcast_to(activations, (NS // 2, *activations.shape))
    same = lax.all_to_all(copies, ("y", "xh"), split_axis=0, concat_axis=0, tiled=True)
    other = swap_cores(same)
    part = dict(zip(ORDER, forward(same, other, w)))
    summed = reduce_over_feat(part)
    recon_error = summed + dec_bias[0].astype(jnp.float32)[None, :] - target[0].astype(jnp.float32)
    blocks = gather_over_feat(narrow(recon_error))
    send, keep = backward(blocks, w)
    pairs = narrow(add(keep, swap_cores(send)))
    arrived = lax.all_to_all(pairs, ("y", "xh"), split_axis=0, concat_axis=0, tiled=True)
    grad_sum = arrived.astype(jnp.float32).sum(axis=0)
    pre_grad = grad_sum * (pre > 0).astype(jnp.float32)
    return recon_error[None], pre_grad[None]


def solution(mesh):
    fine = Mesh(mesh.devices.reshape(4, 2, 2, 2, NZ), (*LAYER, *FEAT))
    return jax.shard_map(
        on_device,
        mesh=fine,
        in_specs=(
            P(LAYER, None, FEAT),
            P(LAYER, None, FEAT, None),
            P(LAYER, FEAT),
            P(LAYER, None, FEAT),
        ),
        out_specs=(P(LAYER, None, FEAT), P(LAYER, None, FEAT)),
        check_vma=False,
    )
```
